32 devices in a mesh: dp: 4 (over z), feat: 8 (over y, x, core).
Axes of the slice: x: 2, y: 2, z: 4, core: 2. Of those that a mesh axis runs over, the one named last changes fastest.
Arguments:
- clip_feats: bfloat16 [2, 384, 8192], P(None, 'dp', 'feat'), may hold values from 0 to 60
- proj_weight: bfloat16 [8192, 8192], P('dp', 'feat'), may hold values from -0.0625 to 0.0625
Outputs:
- loss_value: float32 [], replicated
- weight_grad: float32 [8192, 8192], P('dp', 'feat')
- redundancy: float32 [], replicated
- pair_similarity: float32 [384, 384], P('dp')
The draws below stay inside these ranges and needn't reach their ends.
All inputs are finite; a program needn't handle non-finite values.
Results may differ from the reference program's by a relative error of at most 0.034.
Values may be sent and summed in bfloat16 or wider, within the bound.
A program may use at most 64 MiB of HBM per device.

```python
import math
import jax
import jax.numpy as jnp
from jax import lax

D = 8192
PAIRS_DEV = 96
N = 384
N_DP = 4


def draw_clip_feats(key, part):
    key_base = jax.random.fold_in(key, 11)
    key_noise = jax.random.fold_in(key, 23)
    shared = jax.random.normal(key_base, (N, D), jnp.float32)
    noise = jax.random.normal(key_noise, (2, N, D), jnp.float32)
    values = jnp.clip(shared[None] + 0.5 * noise, 0.0, 6.0)
    return values.astype(jnp.bfloat16)


def steps_of(rng, extent, pieces, low, high):
    level, own = 1.0, jax.random.fold_in(rng, 6)
    for position, shards_of in pieces:
        draws = jnp.exp(jax.random.uniform(jax.random.fold_in(own, position), (shards_of,), jnp.float32, low / len(pieces), high / len(pieces)))
        level = level * jnp.repeat(draws, extent[position] // shards_of).reshape([-1 if axis == position else 1 for axis in range(len(extent))])
    return level


def normal_values(stream_key, dims, width, limit, pieces=(), kind=jnp.bfloat16):
    entries = width * jax.random.normal(stream_key, dims, jnp.float32)
    if pieces:
        entries = entries * steps_of(stream_key, dims, pieces, -0.22, 0.18)
    return jnp.clip(entries, -limit, limit).astype(kind)


def setup_inputs(seed: int = 0) -> dict:
    key_of = jax.random.split(jax.random.key(seed), 3)
    clip_feats = draw_clip_feats(jax.random.fold_in(key_of[2], 71), 0)
    proj_weight = normal_values(key_of[1], (D, D), D ** -0.5, 0.0625, ((0, 4), (1, 8)))
    return {"clip_feats": clip_feats, "proj_weight": proj_weight}


off_weight = 0.0051
epsilon = 1e-05
grad_scale = 32.0

def reference(clip_feats, proj_weight):
    projected = jnp.stack([jnp.dot(clip_feats[0], proj_weight, preferred_element_type=jnp.float32), jnp.dot(clip_feats[1], proj_weight, preferred_element_type=jnp.float32)])
    col_mean = lax.optimization_barrier(jnp.mean(projected, axis=1, keepdims=True))
    centered = projected - col_mean
    col_var = lax.optimization_barrier(jnp.mean(centered * centered, axis=1, keepdims=True))
    col_scale = lax.rsqrt(col_var + epsilon)
    normed = centered * col_scale
    quantized = normed.astype(jnp.bfloat16)
    widened = quantized.astype(jnp.float32)
    pair_count = float(N)
    diag_corr = lax.optimization_barrier(jnp.sum(widened[0] * widened[1], axis=0)) / pair_count
    gram_a = jnp.dot(quantized[0], quantized[0].T, preferred_element_type=jnp.float32)
    gram_b = jnp.dot(quantized[1], quantized[1].T, preferred_element_type=jnp.float32)
    pair_similarity = jnp.where(jnp.eye(N, dtype=bool), 0.0, (gram_a + gram_b) / (2.0 * math.sqrt(float(D))))
    frobenius = jnp.sum(gram_a * gram_b)
    total_loss = jnp.sum((1.0 - diag_corr) ** 2 - off_weight * diag_corr * diag_corr) + off_weight * frobenius / (pair_count * pair_count)
    loss_value = 16.0 * total_loss / float(D)
    off_sum = frobenius / (pair_count * pair_count) - jnp.sum(diag_corr * diag_corr)
    redundancy = 8.0 * pair_count * off_sum / (float(D) * float(D))
    slope = -2.0 * (1.0 - diag_corr) - 2.0 * off_weight * diag_corr
    coefficient = 2.0 * off_weight / (pair_count * pair_count)
    grad_first = slope * widened[1] / pair_count + coefficient * jnp.dot(gram_b.astype(jnp.bfloat16), quantized[0], preferred_element_type=jnp.float32)
    grad_second = slope * widened[0] / pair_count + coefficient * jnp.dot(gram_a.astype(jnp.bfloat16), quantized[1], preferred_element_type=jnp.float32)
    grad_norm = jnp.stack([grad_first, grad_second])
    mean_one = lax.optimization_barrier(jnp.mean(grad_norm, axis=1, keepdims=True))
    mean_two = lax.optimization_barrier(jnp.mean(grad_norm * normed, axis=1, keepdims=True))
    pre_grad = col_scale * (grad_norm - mean_one - normed * mean_two)
    pre_q = pre_grad.astype(jnp.bfloat16)
    rows_blocks = clip_feats.reshape(2, N_DP, PAIRS_DEV, D).transpose(1, 0, 2, 3).reshape(N_DP, 2 * PAIRS_DEV, D)
    grad_blocks = pre_q.reshape(2, N_DP, PAIRS_DEV, D).transpose(1, 0, 2, 3).reshape(N_DP, 2 * PAIRS_DEV, D)

    def add_block(running, blocks):
        rows_blk, grad_blk = blocks
        partial_sum = jnp.dot(rows_blk.T, grad_blk, preferred_element_type=jnp.float32)
        partial_sum = lax.optimization_barrier(partial_sum.astype(jnp.bfloat16)).astype(jnp.float32)
        return (running + partial_sum, None)
    summed, unused = lax.scan(add_block, jnp.zeros((D, D), jnp.float32), (rows_blocks, grad_blocks))
    return (loss_value, grad_scale * summed, redundancy, pair_similarity)
```

```python
import math

import jax
import jax.numpy as jnp
from jax import lax
from jax.sharding import PartitionSpec as P

D = 8192


off_weight = 0.0051
epsilon = 1e-05
grad_scale = 32.0


def per_device(clip_feats, proj_weight):
    pairs = clip_feats.shape[1]
    width = clip_feats.shape[2]
    depth = proj_weight.shape[0]
    dp_count = lax.axis_size("dp")
    total = pairs * dp_count
    pair_count = float(total)
    gathered = lax.all_gather(clip_feats, "feat", axis=0, tiled=False)
    rows = lax.all_to_all(gathered, "dp", split_axis=0, concat_axis=0, tiled=True)
    parts = depth // width
    rows = rows.reshape(dp_count, parts, 2 * pairs, width).transpose(1, 0, 2, 3)
    rows = rows.reshape(parts, 2 * total, width)
    partial = sum(
        jnp.dot(rows[i], proj_weight[i * width : (i + 1) * width], preferred_element_type=jnp.float32)
        for i in range(parts)
    ).reshape(dp_count, 2, pairs, width)
    partial = partial - jnp.mean(partial, axis=(0, 2), keepdims=True)
    columns = width // dp_count
    pieces = partial.astype(jnp.bfloat16).reshape(2 * total, width)
    pieces = jnp.stack([pieces[:, i * columns : (i + 1) * columns] for i in range(dp_count)])
    pieces = lax.all_to_all(pieces, "dp", split_axis=0, concat_axis=0, tiled=True)
    centered = jnp.sum(pieces.astype(jnp.float32), axis=0)
    centered = centered.reshape(dp_count, 2, pairs, columns).transpose(1, 0, 2, 3).reshape(2, total, columns)
    col_var = jnp.mean(centered * centered, axis=1, keepdims=True)
    col_scale = lax.rsqrt(col_var + epsilon)
    normed = centered * col_scale
    quantized = normed.astype(jnp.bfloat16)
    widened = quantized.astype(jnp.float32)
    gram_part = jnp.einsum("vpc,vnc->vpn", quantized, quantized, preferred_element_type=jnp.float32)
    diag_corr = jnp.sum(widened[0] * widened[1], axis=0) / pair_count
    diag_part = jnp.sum((1.0 - diag_corr) ** 2 - off_weight * diag_corr * diag_corr)
    square_part = jnp.sum(diag_corr * diag_corr)
    grams, diag_term, squares = lax.psum((gram_part, diag_part, square_part), ("dp", "feat"))
    frob_scaled = jnp.sum(grams[0] * grams[1]) / (pair_count * pair_count)
    loss_value = 16.0 * (diag_term + off_weight * frob_scaled) / float(D)
    redundancy = 8.0 * pair_count * (frob_scaled - squares) / (float(D) * float(D))
    first_row = lax.axis_index("dp") * pairs
    own = lax.dynamic_slice_in_dim(grams, first_row, pairs, axis=1)
    row_ids = lax.broadcasted_iota(jnp.int32, (pairs, total), 0) + first_row
    col_ids = lax.broadcasted_iota(jnp.int32, (pairs, total), 1)
    pair_similarity = jnp.where(
        row_ids == col_ids, 0.0, (own[0] + own[1]) / (2.0 * math.sqrt(float(D)))
    )
    slope = -2.0 * (1.0 - diag_corr) - 2.0 * off_weight * diag_corr
    coefficient = 2.0 * off_weight / (pair_count * pair_count)
    gram_q = grams.astype(jnp.bfloat16)
    cross_first = jnp.dot(gram_q[1], quantized[0], preferred_element_type=jnp.float32)
    cross_second = jnp.dot(gram_q[0], quantized[1], preferred_element_type=jnp.float32)
    grad_norm = jnp.stack(
        [
            slope * widened[1] / pair_count + coefficient * cross_first,
            slope * widened[0] / pair_count + coefficient * cross_second,
        ]
    )
    mean_one = jnp.mean(grad_norm, axis=1, keepdims=True)
    mean_two = jnp.mean(grad_norm * normed, axis=1, keepdims=True)
    pre_q = (col_scale * (grad_norm - mean_one - normed * mean_two)).astype(jnp.bfloat16)
    pre_q = pre_q.reshape(2, dp_count, pairs, columns).transpose(1, 0, 2, 3).reshape(2 * total, columns)
    flat_grad = lax.all_gather(pre_q, "dp", axis=1, tiled=True)
    summed = jnp.concatenate(
        [jnp.dot(rows[i].T, flat_grad, preferred_element_type=jnp.float32) for i in range(parts)]
    )
    return (loss_value, grad_scale * summed, redundancy, pair_similarity)


def solution(mesh):
    placed = (P(None, "dp", "feat"), P("dp", "feat"))
    return jax.shard_map(
        per_device,
        mesh=mesh,
        in_specs=placed,
        out_specs=(P(), P("dp", "feat"), P(), P("dp", None)),
        check_vma=False,
    )
```

```python
import functools
import math

import jax
import jax.numpy as jnp
from jax import lax
from jax.experimental import pallas as pl
from jax.experimental.pallas import tpu as pltpu
from jax.sharding import PartitionSpec as P

D = 8192


off_weight = 0.0051
epsilon = 1e-05
grad_scale = 32.0

MESH = pl.DeviceIdType.MESH
DMA = pltpu.SemaphoreType.DMA


def remote(src, dst, send_sem, recv_sem, dp, feat):
    return pltpu.make_async_remote_copy(
        src_ref=src,
        dst_ref=dst,
        send_sem=send_sem,
        recv_sem=recv_sem,
        device_id=(dp, feat),
        device_id_type=MESH,
    )


def rows_kernel(n, parts, x_ref, out_ref, send_a, recv_a, send_b, recv_b, send_c, recv_c):
    z, f = lax.axis_index("dp"), lax.axis_index("feat")
    q, c = lax.div(f, parts), lax.rem(f, parts)
    for p in range(n):
        own = jnp.logical_and(z == q, q == p)

        @pl.when(own)
        def _(p=p):
            out_ref[c, p, z] = x_ref[p]

        @pl.when(jnp.logical_not(own))
        def _(p=p):
            remote(x_ref.at[p], out_ref.at[c, p, z], send_a.at[p], recv_a.at[z], q, p * parts + c).start()

    for s in range(n):

        @pl.when(jnp.logical_not(jnp.logical_and(z == q, z == s)))
        def _(s=s):
            remote(x_ref.at[0], out_ref.at[c, q, s], send_a.at[0], recv_a.at[s], z, f).wait_recv()

    def across(d, where):
        block = out_ref.at[c, where]
        return [
            remote(block, block, send_c.at[e, d], recv_c.at[e, d], z, q * parts + lax.rem(c + e, parts))
            for e in range(1, parts)
        ]

    mine = out_ref.at[c, q]
    ring = [
        remote(mine, mine, send_b.at[d], recv_b.at[d], z, lax.rem(q + d, n) * parts + c)
        for d in range(1, n)
    ]
    for copy in ring:
        copy.start()
    pairs = across(0, q)
    for copy in pairs:
        copy.start()
    for d in range(1, n):
        ring[d - 1].wait_recv()
        passed = across(d, lax.rem(q + n - d, n))
        for copy in passed:
            copy.start()
        pairs += passed
    for copy in pairs:
        copy.wait()
    for copy in ring:
        copy.wait_send()
    for p in range(n):

        @pl.when(jnp.logical_not(jnp.logical_and(z == q, q == p)))
        def _(p=p):
            remote(x_ref.at[p], out_ref.at[c, p, z], send_a.at[p], recv_a.at[z], q, p * parts + c).wait_send()


def gram_kernel(
    n, m, g_ref, s_ref, out_ref, total_ref, plane, scalars, mid, scalar_mid, column, scalar_column,
    send_a, recv_a, send_b, recv_b, send_c, recv_c, send_d, recv_d, send_e, recv_e,
):
    z, f = lax.axis_index("dp"), lax.axis_index("feat")
    started = []
    for d in range(1, m):
        to = lax.rem(f + d, m)
        started.append(remote(g_ref.at[to], plane.at[f], send_a.at[d], recv_a.at[d], z, to))
        started.append(remote(s_ref, scalars.at[f], send_b.at[d], recv_b.at[d], z, to))
    for copy in started:
        copy.start()
    plane[f] = g_ref[f]
    scalars[f] = s_ref[...]
    for copy in started:
        copy.wait()
    total = plane[0].astype(jnp.float32)
    for i in range(1, m):
        total += plane[i].astype(jnp.float32)
    mid[...] = total.astype(mid.dtype)
    small = scalars[0]
    for i in range(1, m):
        small += scalars[i]
    scalar_mid[...] = small
    started = []
    for d in range(1, n):
        to = lax.rem(z + d, n)
        started.append(remote(mid, column.at[z], send_c.at[d], recv_c.at[d], to, f))
        started.append(remote(scalar_mid, scalar_column.at[z], send_d.at[d], recv_d.at[d], to, f))
    for copy in started:
        copy.start()
    column[z] = mid[...]
    scalar_column[z] = scalar_mid[...]
    for copy in started:
        copy.wait()
    total = column[0].astype(jnp.float32)
    for i in range(1, n):
        total += column[i].astype(jnp.float32)
    out_ref[f] = total.astype(out_ref.dtype)
    small = scalar_column[0]
    for i in range(1, n):
        small += scalar_column[i]
    total_ref[...] = small
    started = [
        remote(out_ref.at[f], out_ref.at[f], send_e.at[d], recv_e.at[d], z, lax.rem(f + d, m))
        for d in range(1, m)
    ]
    for copy in started:
        copy.start()
    for copy in started:
        copy.wait()


def column_kernel(n, x_ref, out_ref, send_up, recv_up, send_down, recv_down):
    z, f = lax.axis_index("dp"), lax.axis_index("feat")

    def up(d):
        where = out_ref.at[z - d]
        return remote(x_ref if d == 0 else where, where, send_up.at[d], recv_up.at[d], z + 1, f)

    def down(d):
        where = out_ref.at[z + d]
        return remote(x_ref if d == 0 else where, where, send_down.at[d], recv_down.at[d], z - 1, f)

    for d in range(n - 1):
        if d > 0:

            @pl.when(z >= d)
            def _(d=d):
                remote(x_ref, out_ref.at[z - d], send_up.at[0], recv_up.at[d - 1], z, f).wait_recv()

        @pl.when(jnp.logical_and(z >= d, z < n - 1))
        def _(d=d):
            up(d).start()

        if d > 0:

            @pl.when(z + d < n)
            def _(d=d):
                remote(x_ref, out_ref.at[z + d], send_down.at[0], recv_down.at[d - 1], z, f).wait_recv()

        @pl.when(jnp.logical_and(z + d < n, z > 0))
        def _(d=d):
            down(d).start()

    out_ref[z] = x_ref[...]

    @pl.when(z == n - 1)
    def _():
        remote(x_ref, out_ref.at[z - (n - 1)], send_up.at[0], recv_up.at[n - 2], z, f).wait_recv()

    @pl.when(z == 0)
    def _():
        remote(x_ref, out_ref.at[z + (n - 1)], send_down.at[0], recv_down.at[n - 2], z, f).wait_recv()

    for d in range(n - 1):

        @pl.when(jnp.logical_and(z >= d, z < n - 1))
        def _(d=d):
            up(d).wait_send()

        @pl.when(jnp.logical_and(z + d < n, z > 0))
        def _(d=d):
            down(d).wait_send()


def call(kernel, outs, scratch, name, *args):
    return pl.pallas_call(
        kernel,
        out_shape=outs,
        in_specs=[pl.BlockSpec(memory_space=pltpu.VMEM)] * len(args),
        out_specs=jax.tree.map(lambda _: pl.BlockSpec(memory_space=pltpu.VMEM), outs),
        scratch_shapes=scratch,
        compiler_params=pltpu.CompilerParams(has_side_effects=True, vmem_limit_bytes=32 * 2**20),
        name=name,
    )(*args)


def by_kernels(clip_feats, proj_weight):
    pairs = clip_feats.shape[1]
    width = clip_feats.shape[2]
    depth = proj_weight.shape[0]
    n, m = lax.axis_size("dp"), lax.axis_size("feat")
    parts = m // n
    total = pairs * n
    pair_count = float(total)
    columns = width // n
    piece = 2 * pairs // n
    f32, bf16 = jnp.float32, jnp.bfloat16
    rows = call(
        functools.partial(rows_kernel, n, parts),
        jax.ShapeDtypeStruct((parts, n, n, piece, width), bf16),
        [DMA((n,))] * 4 + [DMA((parts, n))] * 2,
        "rows",
        clip_feats.reshape(n, piece, width),
    ).reshape(parts, 2 * total, width)
    partial = sum(
        jnp.dot(rows[i], proj_weight[i * width : (i + 1) * width], preferred_element_type=f32)
        for i in range(parts)
    ).reshape(2, total, width)
    partial = (partial - jnp.mean(partial, axis=1, keepdims=True)).astype(bf16)
    pieces = jnp.stack([partial[:, :, i * columns : (i + 1) * columns] for i in range(n)])
    pieces = lax.all_to_all(pieces, "dp", split_axis=0, concat_axis=0, tiled=True)
    centered = jnp.sum(pieces.astype(f32), axis=0)
    col_var = jnp.mean(centered * centered, axis=1, keepdims=True)
    col_scale = lax.rsqrt(col_var + epsilon)
    normed = centered * col_scale
    quantized = normed.astype(bf16)
    widened = quantized.astype(f32)
    gram_part = jnp.einsum("vpc,vnc->vpn", quantized, quantized, preferred_element_type=f32)
    diag_corr = jnp.sum(widened[0] * widened[1], axis=0) / pair_count
    diag_part = jnp.sum((1.0 - diag_corr) ** 2 - off_weight * diag_corr * diag_corr)
    square_part = jnp.sum(diag_corr * diag_corr)
    lane = lax.broadcasted_iota(jnp.int32, (8, 128), 1)
    small = jnp.where(lane == 0, diag_part, jnp.where(lane == 1, square_part, 0.0))
    block = 2 * total // m
    gram_q, small = call(
        functools.partial(gram_kernel, n, m),
        (jax.ShapeDtypeStruct((m, block, total), bf16), jax.ShapeDtypeStruct((8, 128), f32)),
        [
            pltpu.VMEM((m, block, total), bf16),
            pltpu.VMEM((m, 8, 128), f32),
            pltpu.VMEM((block, total), bf16),
            pltpu.VMEM((8, 128), f32),
            pltpu.VMEM((n, block, total), bf16),
            pltpu.VMEM((n, 8, 128), f32),
        ]
        + [DMA((m,))] * 4
        + [DMA((n,))] * 4
        + [DMA((m,))] * 2,
        "grams",
        gram_part.astype(bf16).reshape(m, block, total),
        small,
    )
    gram_q = gram_q.reshape(2, total, total)
    slope = -2.0 * (1.0 - diag_corr) - 2.0 * off_weight * diag_corr
    coefficient = 2.0 * off_weight / (pair_count * pair_count)
    cross_first = jnp.dot(gram_q[1], quantized[0], preferred_element_type=f32)
    cross_second = jnp.dot(gram_q[0], quantized[1], preferred_element_type=f32)
    grad_norm = jnp.stack(
        [
            slope * widened[1] / pair_count + coefficient * cross_first,
            slope * widened[0] / pair_count + coefficient * cross_second,
        ]
    )
    mean_one = jnp.mean(grad_norm, axis=1, keepdims=True)
    mean_two = jnp.mean(grad_norm * normed, axis=1, keepdims=True)
    pre_q = (col_scale * (grad_norm - mean_one - normed * mean_two)).astype(bf16)
    flat_grad = call(
        functools.partial(column_kernel, n),
        jax.ShapeDtypeStruct((n, 2 * total, columns), bf16),
        [DMA((n,))] * 4,
        "columns",
        pre_q.reshape(2 * total, columns),
    )
    flat_grad = jnp.concatenate([flat_grad[i] for i in range(n)], axis=1)
    summed = jnp.einsum("crk,rw->ckw", rows, flat_grad, preferred_element_type=f32)
    weight_grad = grad_scale * summed.reshape(depth, width)
    grams = gram_q.astype(f32)
    frob_scaled = jnp.sum(grams[0] * grams[1]) / (pair_count * pair_count)
    loss_value = 16.0 * (small[0, 0] + off_weight * frob_scaled) / float(D)
    redundancy = 8.0 * pair_count * (frob_scaled - small[0, 1]) / (float(D) * float(D))
    half = n // 2
    z = lax.axis_index("dp")
    own = grams.reshape(2, half, n, piece, total)
    own = lax.dynamic_slice_in_dim(own, z, 1, axis=2)
    own = (own[0] + own[1]).reshape(pairs, half, n, piece).transpose(0, 2, 1, 3).reshape(pairs, total)
    row_ids = lax.broadcasted_iota(jnp.int32, (pairs, total), 0) + z * pairs
    col_ids = lax.broadcasted_iota(jnp.int32, (pairs, total), 1)
    pair_similarity = jnp.where(row_ids == col_ids, 0.0, own / (2.0 * math.sqrt(float(D))))
    return (loss_value, weight_grad, redundancy, pair_similarity)


def by_collectives(clip_feats, proj_weight):
    pairs = clip_feats.shape[1]
    width = clip_feats.shape[2]
    depth = proj_weight.shape[0]
    dp_count = lax.axis_size("dp")
    total = pairs * dp_count
    pair_count = float(total)
    gathered = lax.all_gather(clip_feats, "feat", axis=0, tiled=False)
    rows = lax.all_to_all(gathered, "dp", split_axis=0, concat_axis=0, tiled=True)
    parts = depth // width
    rows = rows.reshape(dp_count, parts, 2 * pairs, width).transpose(1, 0, 2, 3)
    rows = rows.reshape(parts, 2 * total, width)
    partial = sum(
        jnp.dot(rows[i], proj_weight[i * width : (i + 1) * width], preferred_element_type=jnp.float32)
        for i in range(parts)
    ).reshape(dp_count, 2, pairs, width)
    partial = partial - jnp.mean(partial, axis=(0, 2), keepdims=True)
    columns = width // dp_count
    pieces = partial.astype(jnp.bfloat16).reshape(2 * total, width)
    pieces = jnp.stack([pieces[:, i * columns : (i + 1) * columns] for i in range(dp_count)])
    pieces = lax.all_to_all(pieces, "dp", split_axis=0, concat_axis=0, tiled=True)
    centered = jnp.sum(pieces.astype(jnp.float32), axis=0)
    centered = centered.reshape(dp_count, 2, pairs, columns).transpose(1, 0, 2, 3).reshape(2, total, columns)
    col_var = jnp.mean(centered * centered, axis=1, keepdims=True)
    col_scale = lax.rsqrt(col_var + epsilon)
    normed = centered * col_scale
    quantized = normed.astype(jnp.bfloat16)
    widened = quantized.astype(jnp.float32)
    gram_part = jnp.einsum("vpc,vnc->vpn", quantized, quantized, preferred_element_type=jnp.float32)
    diag_corr = jnp.sum(widened[0] * widened[1], axis=0) / pair_count
    diag_part = jnp.sum((1.0 - diag_corr) ** 2 - off_weight * diag_corr * diag_corr)
    square_part = jnp.sum(diag_corr * diag_corr)
    grams, diag_term, squares = lax.psum((gram_part, diag_part, square_part), ("dp", "feat"))
    frob_scaled = jnp.sum(grams[0] * grams[1]) / (pair_count * pair_count)
    loss_value = 16.0 * (diag_term + off_weight * frob_scaled) / float(D)
    redundancy = 8.0 * pair_count * (frob_scaled - squares) / (float(D) * float(D))
    first_row = lax.axis_index("dp") * pairs
    own = lax.dynamic_slice_in_dim(grams, first_row, pairs, axis=1)
    row_ids = lax.broadcasted_iota(jnp.int32, (pairs, total), 0) + first_row
    col_ids = lax.broadcasted_iota(jnp.int32, (pairs, total), 1)
    pair_similarity = jnp.where(
        row_ids == col_ids, 0.0, (own[0] + own[1]) / (2.0 * math.sqrt(float(D)))
    )
    slope = -2.0 * (1.0 - diag_corr) - 2.0 * off_weight * diag_corr
    coefficient = 2.0 * off_weight / (pair_count * pair_count)
    gram_q = grams.astype(jnp.bfloat16)
    cross_first = jnp.dot(gram_q[1], quantized[0], preferred_element_type=jnp.float32)
    cross_second = jnp.dot(gram_q[0], quantized[1], preferred_element_type=jnp.float32)
    grad_norm = jnp.stack(
        [
            slope * widened[1] / pair_count + coefficient * cross_first,
            slope * widened[0] / pair_count + coefficient * cross_second,
        ]
    )
    mean_one = jnp.mean(grad_norm, axis=1, keepdims=True)
    mean_two = jnp.mean(grad_norm * normed, axis=1, keepdims=True)
    pre_q = (col_scale * (grad_norm - mean_one - normed * mean_two)).astype(jnp.bfloat16)
    pre_q = pre_q.reshape(2, dp_count, pairs, columns).transpose(1, 0, 2, 3).reshape(2 * total, columns)
    flat_grad = lax.all_gather(pre_q, "dp", axis=1, tiled=True)
    summed = jnp.concatenate(
        [jnp.dot(rows[i].T, flat_grad, preferred_element_type=jnp.float32) for i in range(parts)]
    )
    return (loss_value, grad_scale * summed, redundancy, pair_similarity)


def per_device(clip_feats, proj_weight):
    pairs, width = clip_feats.shape[1:]
    n, m = lax.axis_size("dp"), lax.axis_size("feat")
    aligned = n % 2 == 0 and m % n == 0 and m > n and proj_weight.shape[0] == width * (m // n)
    aligned = aligned and width % (128 * n) == 0 and (2 * pairs) % (16 * n) == 0
    aligned = aligned and (2 * pairs * n) % (16 * m) == 0
    return (by_kernels if aligned else by_collectives)(clip_feats, proj_weight)


def solution(mesh):
    placed = (P(None, "dp", "feat"), P("dp", "feat"))
    return jax.shard_map(
        per_device,
        mesh=mesh,
        in_specs=placed,
        out_specs=(P(), P("dp", "feat"), P(), P("dp", None)),
        check_vma=False,
    )
```

```python
import functools
import math

import jax
import jax.numpy as jnp
from jax import lax
from jax.experimental import pallas as pl
from jax.experimental.pallas import tpu as pltpu
from jax.sharding import PartitionSpec as P

D = 8192


off_weight = 0.0051
epsilon = 1e-05
grad_scale = 32.0
cuts = 4

MESH = pl.DeviceIdType.MESH
DMA = pltpu.SemaphoreType.DMA


def remote(src, dst, send_sem, recv_sem, dp, feat):
    return pltpu.make_async_remote_copy(
        src_ref=src,
        dst_ref=dst,
        send_sem=send_sem,
        recv_sem=recv_sem,
        device_id=(dp, feat),
        device_id_type=MESH,
    )


def rows_kernel(
    n, parts, x_ref, out_ref, mid, local, send_a, recv_a, send_b, recv_b, send_c, recv_c, send_d, recv_d
):
    z, f = lax.axis_index("dp"), lax.axis_index("feat")
    q, c = lax.div(f, parts), lax.rem(f, parts)
    spread = []
    for d in range(1, n):
        to = lax.rem(q + d, n)
        spread.append(remote(x_ref.at[to], mid.at[q], send_a.at[d], recv_a.at[d], z, to * parts + c))
    for copy in spread:
        copy.start()
    kept = pltpu.make_async_copy(x_ref.at[q], mid.at[q], local.at[0])
    kept.start()
    kept.wait()
    for d in range(n):
        s = lax.rem(q + n - d, n)
        if d > 0:
            spread[d - 1].wait_recv()

        @pl.when(z != s)
        def _(d=d, s=s):
            remote(mid.at[s], out_ref.at[c, q, z], send_b.at[d], recv_b.at[z], s, f).start()

        @pl.when(z == s)
        def _(s=s):
            own = pltpu.make_async_copy(mid.at[s], out_ref.at[c, q, z], local.at[1])
            own.start()
            own.wait()

    def across(d, e):
        block = out_ref.at[c, lax.rem(q + n - d, n), lax.rem(z + e, n)]
        return [
            remote(block, block, send_d.at[i, d, e], recv_d.at[i, d, e], z, q * parts + lax.rem(c + i, parts))
            for i in range(1, parts)
        ]

    ring, pairs = {}, []
    for e in range(n):
        s = lax.rem(z + e, n)
        mine = out_ref.at[c, q, s]
        if e > 0:
            remote(x_ref.at[0], mine, send_b.at[0], recv_b.at[s], z, f).wait_recv()
        for d in range(1, n):
            to = lax.rem(q + d, n) * parts + c
            ring[d, e] = remote(mine, mine, send_c.at[d, e], recv_c.at[d, e], z, to)
            ring[d, e].start()
        passed = across(0, e)
        for copy in passed:
            copy.start()
        pairs += passed
    for e in range(n):
        for d in range(1, n):
            ring[d, e].wait_recv()
            passed = across(d, e)
            for copy in passed:
                copy.start()
            pairs += passed
    for copy in pairs:
        copy.wait()
    for copy in list(ring.values()) + spread:
        copy.wait_send()
    for d in range(n):
        s = lax.rem(q + n - d, n)

        @pl.when(z != s)
        def _(d=d, s=s):
            remote(mid.at[s], out_ref.at[c, q, z], send_b.at[d], recv_b.at[z], s, f).wait_send()


def sums_kernel(n, k, x_ref, out_ref, sums, above, below, send_up, recv_up, send_down, recv_down):
    z, f = lax.axis_index("dp"), lax.axis_index("feat")

    def step(t, i, start, rising):
        first = z == (0 if rising else n - 1)
        active = z < t if rising else z > t
        got = below if rising else above
        send, recv = (send_up, recv_up) if rising else (send_down, recv_down)
        to = z + 1 if rising else z - 1

        @pl.when(jnp.logical_and(active, first))
        def _():
            copy = remote(x_ref.at[t, i], got.at[t, i], send.at[t, i], recv.at[t, i], to, f)
            copy.start() if start else copy.wait_send()

        @pl.when(jnp.logical_and(active, jnp.logical_not(first)))
        def _():
            copy = remote(sums.at[t, i], got.at[t, i], send.at[t, i], recv.at[t, i], to, f)
            if start:
                copy.wait_recv()
                total = x_ref[t, i].astype(jnp.float32) + got[t, i].astype(jnp.float32)
                sums[t, i] = total.astype(sums.dtype)
                copy.start()
            else:
                copy.wait_send()

    for j in range(n - 1):
        for i in range(k):
            step(n - 1 - j, i, True, True)
            step(j, i, True, False)
    out_ref[...] = x_ref[z].astype(jnp.float32)
    for i in range(k):

        @pl.when(z > 0)
        def _(i=i):
            remote(x_ref.at[0, i], below.at[z, i], send_up.at[0, i], recv_up.at[z, i], z, f).wait_recv()
            out_ref[i] += below[z, i].astype(jnp.float32)

        @pl.when(z < n - 1)
        def _(i=i):
            remote(x_ref.at[0, i], above.at[z, i], send_down.at[0, i], recv_down.at[z, i], z, f).wait_recv()
            out_ref[i] += above[z, i].astype(jnp.float32)

    for j in range(n - 1):
        for i in range(k):
            step(n - 1 - j, i, False, True)
            step(j, i, False, False)


def gram_kernel(
    n, m, g_ref, s_ref, out_ref, total_ref, plane, scalars, mid, scalar_mid, column, scalar_column,
    send_a, recv_a, send_b, recv_b, send_c, recv_c, send_d, recv_d, send_e, recv_e,
):
    z, f = lax.axis_index("dp"), lax.axis_index("feat")
    started = []
    for d in range(1, m):
        to = lax.rem(f + d, m)
        started.append(remote(g_ref.at[to], plane.at[f], send_a.at[d], recv_a.at[d], z, to))
        started.append(remote(s_ref, scalars.at[f], send_b.at[d], recv_b.at[d], z, to))
    for copy in started:
        copy.start()
    plane[f] = g_ref[f]
    scalars[f] = s_ref[...]
    for copy in started:
        copy.wait()
    total = plane[0].astype(jnp.float32)
    for i in range(1, m):
        total += plane[i].astype(jnp.float32)
    mid[...] = total.astype(mid.dtype)
    small = scalars[0]
    for i in range(1, m):
        small += scalars[i]
    scalar_mid[...] = small
    started = []
    for d in range(1, n):
        to = lax.rem(z + d, n)
        started.append(remote(mid, column.at[z], send_c.at[d], recv_c.at[d], to, f))
        started.append(remote(scalar_mid, scalar_column.at[z], send_d.at[d], recv_d.at[d], to, f))
    for copy in started:
        copy.start()
    column[z] = mid[...]
    scalar_column[z] = scalar_mid[...]
    for copy in started:
        copy.wait()
    total = column[0].astype(jnp.float32)
    for i in range(1, n):
        total += column[i].astype(jnp.float32)
    out_ref[f] = total.astype(out_ref.dtype)
    small = scalar_column[0]
    for i in range(1, n):
        small += scalar_column[i]
    total_ref[...] = small
    started = [
        remote(out_ref.at[f], out_ref.at[f], send_e.at[d], recv_e.at[d], z, lax.rem(f + d, m))
        for d in range(1, m)
    ]
    for copy in started:
        copy.start()
    for copy in started:
        copy.wait()


def column_kernel(n, k, x_ref, out_ref, send_up, recv_up, send_down, recv_down):
    z, f = lax.axis_index("dp"), lax.axis_index("feat")

    def up(d, i):
        where = out_ref.at[z - d, i]
        src = x_ref.at[i] if d == 0 else where
        return remote(src, where, send_up.at[d, i], recv_up.at[d, i], z + 1, f)

    def down(d, i):
        where = out_ref.at[z + d, i]
        src = x_ref.at[i] if d == 0 else where
        return remote(src, where, send_down.at[d, i], recv_down.at[d, i], z - 1, f)

    def arrived(d, i):
        @pl.when(z >= d)
        def _():
            remote(x_ref.at[i], out_ref.at[z - d, i], send_up.at[0, i], recv_up.at[d - 1, i], z, f).wait_recv()

        @pl.when(z + d < n)
        def _():
            remote(x_ref.at[i], out_ref.at[z + d, i], send_down.at[0, i], recv_down.at[d - 1, i], z, f).wait_recv()

    for d in range(n - 1):
        for i in range(k):
            if d > 0:
                arrived(d, i)

            @pl.when(jnp.logical_and(z >= d, z < n - 1))
            def _(d=d, i=i):
                up(d, i).start()

            @pl.when(jnp.logical_and(z + d < n, z > 0))
            def _(d=d, i=i):
                down(d, i).start()

    out_ref[z] = x_ref[...]
    for i in range(k):
        arrived(n - 1, i)
    for d in range(n - 1):
        for i in range(k):

            @pl.when(jnp.logical_and(z >= d, z < n - 1))
            def _(d=d, i=i):
                up(d, i).wait_send()

            @pl.when(jnp.logical_and(z + d < n, z > 0))
            def _(d=d, i=i):
                down(d, i).wait_send()


def call(kernel, outs, scratch, name, *args):
    return pl.pallas_call(
        kernel,
        out_shape=outs,
        in_specs=[pl.BlockSpec(memory_space=pltpu.VMEM)] * len(args),
        out_specs=jax.tree.map(lambda _: pl.BlockSpec(memory_space=pltpu.VMEM), outs),
        scratch_shapes=scratch,
        compiler_params=pltpu.CompilerParams(has_side_effects=True, vmem_limit_bytes=32 * 2**20),
        name=name,
    )(*args)


def by_kernels(clip_feats, proj_weight):
    pairs = clip_feats.shape[1]
    width = clip_feats.shape[2]
    depth = proj_weight.shape[0]
    n, m = lax.axis_size("dp"), lax.axis_size("feat")
    parts = m // n
    total = pairs * n
    pair_count = float(total)
    columns = width // n
    piece = 2 * pairs // n
    f32, bf16 = jnp.float32, jnp.bfloat16
    rows = call(
        functools.partial(rows_kernel, n, parts),
        jax.ShapeDtypeStruct((parts, n, n, piece, width), bf16),
        [pltpu.VMEM((n, piece, width), bf16), DMA((2,))]
        + [DMA((n,))] * 4
        + [DMA((n, n))] * 2
        + [DMA((parts, n, n))] * 2,
        "rows",
        clip_feats.reshape(n, piece, width),
    ).reshape(parts, 2 * total, width)
    partial = sum(
        jnp.dot(rows[i], proj_weight[i * width : (i + 1) * width], preferred_element_type=f32)
        for i in range(parts)
    ).reshape(2, total, width)
    partial = (partial - jnp.mean(partial, axis=1, keepdims=True)).astype(bf16)
    pieces = jnp.stack([partial[:, :, i * columns : (i + 1) * columns] for i in range(n)])
    k = cuts
    centered = call(
        functools.partial(sums_kernel, n, k),
        jax.ShapeDtypeStruct((k, 2 * total // k, columns), f32),
        [pltpu.VMEM((n, k, 2 * total // k, columns), bf16)] * 3 + [DMA((n, k))] * 4,
        "sums",
        pieces.reshape(n, k, 2 * total // k, columns),
    ).reshape(2, total, columns)
    col_var = jnp.mean(centered * centered, axis=1, keepdims=True)
    col_scale = lax.rsqrt(col_var + epsilon)
    normed = centered * col_scale
    quantized = normed.astype(bf16)
    widened = quantized.astype(f32)
    gram_part = jnp.einsum("vpc,vnc->vpn", quantized, quantized, preferred_element_type=f32)
    diag_corr = jnp.sum(widened[0] * widened[1], axis=0) / pair_count
    diag_part = jnp.sum((1.0 - diag_corr) ** 2 - off_weight * diag_corr * diag_corr)
    square_part = jnp.sum(diag_corr * diag_corr)
    lane = lax.broadcasted_iota(jnp.int32, (8, 128), 1)
    small = jnp.where(lane == 0, diag_part, jnp.where(lane == 1, square_part, 0.0))
    block = 2 * total // m
    gram_q, small = call(
        functools.partial(gram_kernel, n, m),
        (jax.ShapeDtypeStruct((m, block, total), bf16), jax.ShapeDtypeStruct((8, 128), f32)),
        [
            pltpu.VMEM((m, block, total), bf16),
            pltpu.VMEM((m, 8, 128), f32),
            pltpu.VMEM((block, total), bf16),
            pltpu.VMEM((8, 128), f32),
            pltpu.VMEM((n, block, total), bf16),
            pltpu.VMEM((n, 8, 128), f32),
        ]
        + [DMA((m,))] * 4
        + [DMA((n,))] * 4
        + [DMA((m,))] * 2,
        "grams",
        gram_part.astype(bf16).reshape(m, block, total),
        small,
    )
    gram_q = gram_q.reshape(2, total, total)
    slope = -2.0 * (1.0 - diag_corr) - 2.0 * off_weight * diag_corr
    coefficient = 2.0 * off_weight / (pair_count * pair_count)
    cross_first = jnp.dot(gram_q[1], quantized[0], preferred_element_type=f32)
    cross_second = jnp.dot(gram_q[0], quantized[1], preferred_element_type=f32)
    grad_norm = jnp.stack(
        [
            slope * widened[1] / pair_count + coefficient * cross_first,
            slope * widened[0] / pair_count + coefficient * cross_second,
        ]
    )
    mean_one = jnp.mean(grad_norm, axis=1, keepdims=True)
    mean_two = jnp.mean(grad_norm * normed, axis=1, keepdims=True)
    pre_q = (col_scale * (grad_norm - mean_one - normed * mean_two)).astype(bf16)
    flat_grad = call(
        functools.partial(column_kernel, n, k),
        jax.ShapeDtypeStruct((n, k, 2 * total // k, columns), bf16),
        [DMA((n, k))] * 4,
        "columns",
        pre_q.reshape(k, 2 * total // k, columns),
    ).reshape(n, 2 * total, columns)
    flat_grad = jnp.concatenate([flat_grad[i] for i in range(n)], axis=1)
    summed = jnp.einsum("crk,rw->ckw", rows, flat_grad, preferred_element_type=f32)
    weight_grad = grad_scale * summed.reshape(depth, width)
    grams = gram_q.astype(f32)
    frob_scaled = jnp.sum(grams[0] * grams[1]) / (pair_count * pair_count)
    loss_value = 16.0 * (small[0, 0] + off_weight * frob_scaled) / float(D)
    redundancy = 8.0 * pair_count * (frob_scaled - small[0, 1]) / (float(D) * float(D))
    half = n // 2
    z = lax.axis_index("dp")
    own = grams.reshape(2, half, n, piece, total)
    own = lax.dynamic_slice_in_dim(own, z, 1, axis=2)
    own = (own[0] + own[1]).reshape(pairs, half, n, piece).transpose(0, 2, 1, 3).reshape(pairs, total)
    row_ids = lax.broadcasted_iota(jnp.int32, (pairs, total), 0) + z * pairs
    col_ids = lax.broadcasted_iota(jnp.int32, (pairs, total), 1)
    pair_similarity = jnp.where(row_ids == col_ids, 0.0, own / (2.0 * math.sqrt(float(D))))
    return (loss_value, weight_grad, redundancy, pair_similarity)


def by_collectives(clip_feats, proj_weight):
    pairs = clip_feats.shape[1]
    width = clip_feats.shape[2]
    depth = proj_weight.shape[0]
    dp_count = lax.axis_size("dp")
    total = pairs * dp_count
    pair_count = float(total)
    gathered = lax.all_gather(clip_feats, "feat", axis=0, tiled=False)
    rows = lax.all_to_all(gathered, "dp", split_axis=0, concat_axis=0, tiled=True)
    parts = depth // width
    rows = rows.reshape(dp_count, parts, 2 * pairs, width).transpose(1, 0, 2, 3)
    rows = rows.reshape(parts, 2 * total, width)
    partial = sum(
        jnp.dot(rows[i], proj_weight[i * width : (i + 1) * width], preferred_element_type=jnp.float32)
        for i in range(parts)
    ).reshape(dp_count, 2, pairs, width)
    partial = partial - jnp.mean(partial, axis=(0, 2), keepdims=True)
    columns = width // dp_count
    pieces = partial.astype(jnp.bfloat16).reshape(2 * total, width)
    pieces = jnp.stack([pieces[:, i * columns : (i + 1) * columns] for i in range(dp_count)])
    pieces = lax.all_to_all(pieces, "dp", split_axis=0, concat_axis=0, tiled=True)
    centered = jnp.sum(pieces.astype(jnp.float32), axis=0)
    centered = centered.reshape(dp_count, 2, pairs, columns).transpose(1, 0, 2, 3).reshape(2, total, columns)
    col_var = jnp.mean(centered * centered, axis=1, keepdims=True)
    col_scale = lax.rsqrt(col_var + epsilon)
    normed = centered * col_scale
    quantized = normed.astype(jnp.bfloat16)
    widened = quantized.astype(jnp.float32)
    gram_part = jnp.einsum("vpc,vnc->vpn", quantized, quantized, preferred_element_type=jnp.float32)
    diag_corr = jnp.sum(widened[0] * widened[1], axis=0) / pair_count
    diag_part = jnp.sum((1.0 - diag_corr) ** 2 - off_weight * diag_corr * diag_corr)
    square_part = jnp.sum(diag_corr * diag_corr)
    grams, diag_term, squares = lax.psum((gram_part, diag_part, square_part), ("dp", "feat"))
    frob_scaled = jnp.sum(grams[0] * grams[1]) / (pair_count * pair_count)
    loss_value = 16.0 * (diag_term + off_weight * frob_scaled) / float(D)
    redundancy = 8.0 * pair_count * (frob_scaled - squares) / (float(D) * float(D))
    first_row = lax.axis_index("dp") * pairs
    own = lax.dynamic_slice_in_dim(grams, first_row, pairs, axis=1)
    row_ids = lax.broadcasted_iota(jnp.int32, (pairs, total), 0) + first_row
    col_ids = lax.broadcasted_iota(jnp.int32, (pairs, total), 1)
    pair_similarity = jnp.where(
        row_ids == col_ids, 0.0, (own[0] + own[1]) / (2.0 * math.sqrt(float(D)))
    )
    slope = -2.0 * (1.0 - diag_corr) - 2.0 * off_weight * diag_corr
    coefficient = 2.0 * off_weight / (pair_count * pair_count)
    gram_q = grams.astype(jnp.bfloat16)
    cross_first = jnp.dot(gram_q[1], quantized[0], preferred_element_type=jnp.float32)
    cross_second = jnp.dot(gram_q[0], quantized[1], preferred_element_type=jnp.float32)
    grad_norm = jnp.stack(
        [
            slope * widened[1] / pair_count + coefficient * cross_first,
            slope * widened[0] / pair_count + coefficient * cross_second,
        ]
    )
    mean_one = jnp.mean(grad_norm, axis=1, keepdims=True)
    mean_two = jnp.mean(grad_norm * normed, axis=1, keepdims=True)
    pre_q = (col_scale * (grad_norm - mean_one - normed * mean_two)).astype(jnp.bfloat16)
    pre_q = pre_q.reshape(2, dp_count, pairs, columns).transpose(1, 0, 2, 3).reshape(2 * total, columns)
    flat_grad = lax.all_gather(pre_q, "dp", axis=1, tiled=True)
    summed = jnp.concatenate(
        [jnp.dot(rows[i].T, flat_grad, preferred_element_type=jnp.float32) for i in range(parts)]
    )
    return (loss_value, grad_scale * summed, redundancy, pair_similarity)


def per_device(clip_feats, proj_weight):
    pairs, width = clip_feats.shape[1:]
    n, m = lax.axis_size("dp"), lax.axis_size("feat")
    aligned = n % 2 == 0 and m % n == 0 and m > n and proj_weight.shape[0] == width * (m // n)
    aligned = aligned and width % (128 * n) == 0 and (2 * pairs) % (16 * n) == 0
    aligned = aligned and (2 * pairs * n) % (16 * m) == 0
    aligned = aligned and (2 * pairs * n) % (16 * cuts) == 0
    return (by_kernels if aligned else by_collectives)(clip_feats, proj_weight)


def solution(mesh):
    placed = (P(None, "dp", "feat"), P("dp", "feat"))
    return jax.shard_map(
        per_device,
        mesh=mesh,
        in_specs=placed,
        out_specs=(P(), P("dp", "feat"), P(), P("dp", None)),
        check_vma=False,
    )
```

```python
import functools
import math

import jax
import jax.numpy as jnp
from jax import lax
from jax.experimental import pallas as pl
from jax.experimental.pallas import tpu as pltpu
from jax.sharding import PartitionSpec as P

D = 8192


off_weight = 0.0051
epsilon = 1e-05
grad_scale = 32.0
cuts = 4

MESH = pl.DeviceIdType.MESH
DMA = pltpu.SemaphoreType.DMA


def remote(src, dst, send_sem, recv_sem, dp, feat):
    return pltpu.make_async_remote_copy(
        src_ref=src,
        dst_ref=dst,
        send_sem=send_sem,
        recv_sem=recv_sem,
        device_id=(dp, feat),
        device_id_type=MESH,
    )


def rows_kernel(
    n, parts, x_ref, out_ref, mid, local, send_a, recv_a, send_b, recv_b, send_c, recv_c, send_d, recv_d
):
    z, f = lax.axis_index("dp"), lax.axis_index("feat")
    q, c = lax.div(f, parts), lax.rem(f, parts)
    spread = []
    for d in range(1, n):
        to = lax.rem(q + d, n)
        spread.append(remote(x_ref.at[to], mid.at[q], send_a.at[d], recv_a.at[d], z, to * parts + c))
    for copy in spread:
        copy.start()
    kept = pltpu.make_async_copy(x_ref.at[q], mid.at[q], local.at[0])
    kept.start()
    kept.wait()
    for d in range(n):
        s = lax.rem(q + n - d, n)
        if d > 0:
            spread[d - 1].wait_recv()

        @pl.when(z != s)
        def _(d=d, s=s):
            remote(mid.at[s], out_ref.at[c, q, z], send_b.at[d], recv_b.at[z], s, f).start()

        @pl.when(z == s)
        def _(s=s):
            own = pltpu.make_async_copy(mid.at[s], out_ref.at[c, q, z], local.at[1])
            own.start()
            own.wait()

    def across(d, e):
        block = out_ref.at[c, lax.rem(q + n - d, n), lax.rem(z + e, n)]
        return [
            remote(block, block, send_d.at[i, d, e], recv_d.at[i, d, e], z, q * parts + lax.rem(c + i, parts))
            for i in range(1, parts)
        ]

    ring, pairs = {}, []
    for e in range(n):
        s = lax.rem(z + e, n)
        mine = out_ref.at[c, q, s]
        if e > 0:
            remote(x_ref.at[0], mine, send_b.at[0], recv_b.at[s], z, f).wait_recv()
        for d in range(1, n):
            to = lax.rem(q + d, n) * parts + c
            ring[d, e] = remote(mine, mine, send_c.at[d, e], recv_c.at[d, e], z, to)
            ring[d, e].start()
        passed = across(0, e)
        for copy in passed:
            copy.start()
        pairs += passed
    for e in range(n):
        for d in range(1, n):
            ring[d, e].wait_recv()
            passed = across(d, e)
            for copy in passed:
                copy.start()
            pairs += passed
    for copy in pairs:
        copy.wait()
    for copy in list(ring.values()) + spread:
        copy.wait_send()
    for d in range(n):
        s = lax.rem(q + n - d, n)

        @pl.when(z != s)
        def _(d=d, s=s):
            remote(mid.at[s], out_ref.at[c, q, z], send_b.at[d], recv_b.at[z], s, f).wait_send()


def sums_kernel(n, k, x_ref, out_ref, sums, above, below, send_up, recv_up, send_down, recv_down):
    z, f = lax.axis_index("dp"), lax.axis_index("feat")

    def step(t, i, start, rising):
        first = z == (0 if rising else n - 1)
        active = z < t if rising else z > t
        got = below if rising else above
        send, recv = (send_up, recv_up) if rising else (send_down, recv_down)
        to = z + 1 if rising else z - 1

        @pl.when(jnp.logical_and(active, first))
        def _():
            copy = remote(x_ref.at[t, i], got.at[t, i], send.at[t, i], recv.at[t, i], to, f)
            order = (n - 1 - t if rising else t) * k + i
            if start:
                copy.start()
                if order >= 2:
                    j, b = divmod(order - 2, k)
                    a = n - 1 - j if rising else j
                    remote(x_ref.at[a, b], got.at[a, b], send.at[a, b], recv.at[a, b], to, f).wait_send()
            elif order >= (n - 1) * k - 2:
                copy.wait_send()

        @pl.when(jnp.logical_and(active, jnp.logical_not(first)))
        def _():
            copy = remote(sums.at[t, i], got.at[t, i], send.at[t, i], recv.at[t, i], to, f)
            if start:
                copy.wait_recv()
                total = x_ref[t, i].astype(jnp.float32) + got[t, i].astype(jnp.float32)
                sums[t, i] = total.astype(sums.dtype)
                copy.start()
            else:
                copy.wait_send()

    for j in range(n - 1):
        for i in range(k):
            step(n - 1 - j, i, True, True)
            step(j, i, True, False)
    out_ref[...] = x_ref[z].astype(jnp.float32)
    for i in range(k):

        @pl.when(z > 0)
        def _(i=i):
            remote(x_ref.at[0, i], below.at[z, i], send_up.at[0, i], recv_up.at[z, i], z, f).wait_recv()
            out_ref[i] += below[z, i].astype(jnp.float32)

        @pl.when(z < n - 1)
        def _(i=i):
            remote(x_ref.at[0, i], above.at[z, i], send_down.at[0, i], recv_down.at[z, i], z, f).wait_recv()
            out_ref[i] += above[z, i].astype(jnp.float32)

    for j in range(n - 1):
        for i in range(k):
            step(n - 1 - j, i, False, True)
            step(j, i, False, False)


def gram_kernel(
    n, m, g_ref, s_ref, out_ref, total_ref, plane, scalars, mid, scalar_mid, column, scalar_column,
    send_a, recv_a, send_b, recv_b, send_c, recv_c, send_d, recv_d, send_e, recv_e,
):
    z, f = lax.axis_index("dp"), lax.axis_index("feat")
    started = []
    for d in range(1, m):
        to = lax.rem(f + d, m)
        started.append(remote(g_ref.at[to], plane.at[f], send_a.at[d], recv_a.at[d], z, to))
        started.append(remote(s_ref, scalars.at[f], send_b.at[d], recv_b.at[d], z, to))
    for copy in started:
        copy.start()
    plane[f] = g_ref[f]
    scalars[f] = s_ref[...]
    for copy in started:
        copy.wait()
    total = plane[0].astype(jnp.float32)
    for i in range(1, m):
        total += plane[i].astype(jnp.float32)
    mid[...] = total.astype(mid.dtype)
    small = scalars[0]
    for i in range(1, m):
        small += scalars[i]
    scalar_mid[...] = small
    started = []
    for d in range(1, n):
        to = lax.rem(z + d, n)
        started.append(remote(mid, column.at[z], send_c.at[d], recv_c.at[d], to, f))
        started.append(remote(scalar_mid, scalar_column.at[z], send_d.at[d], recv_d.at[d], to, f))
    for copy in started:
        copy.start()
    column[z] = mid[...]
    scalar_column[z] = scalar_mid[...]
    for copy in started:
        copy.wait()
    total = column[0].astype(jnp.float32)
    for i in range(1, n):
        total += column[i].astype(jnp.float32)
    out_ref[f] = total.astype(out_ref.dtype)
    small = scalar_column[0]
    for i in range(1, n):
        small += scalar_column[i]
    total_ref[...] = small
    started = [
        remote(out_ref.at[f], out_ref.at[f], send_e.at[d], recv_e.at[d], z, lax.rem(f + d, m))
        for d in range(1, m)
    ]
    for copy in started:
        copy.start()
    for copy in started:
        copy.wait()


def column_kernel(n, k, x_ref, out_ref, send_up, recv_up, send_down, recv_down):
    z, f = lax.axis_index("dp"), lax.axis_index("feat")

    def up(d, i):
        where = out_ref.at[z - d, i]
        src = x_ref.at[i] if d == 0 else where
        return remote(src, where, send_up.at[d, i], recv_up.at[d, i], z + 1, f)

    def down(d, i):
        where = out_ref.at[z + d, i]
        src = x_ref.at[i] if d == 0 else where
        return remote(src, where, send_down.at[d, i], recv_down.at[d, i], z - 1, f)

    def arrived(d, i):
        @pl.when(z >= d)
        def _():
            remote(x_ref.at[i], out_ref.at[z - d, i], send_up.at[0, i], recv_up.at[d - 1, i], z, f).wait_recv()

        @pl.when(z + d < n)
        def _():
            remote(x_ref.at[i], out_ref.at[z + d, i], send_down.at[0, i], recv_down.at[d - 1, i], z, f).wait_recv()

    for d in range(n - 1):
        for i in range(k):
            if d > 0:
                arrived(d, i)

            @pl.when(jnp.logical_and(z >= d, z < n - 1))
            def _(d=d, i=i):
                up(d, i).start()

            @pl.when(jnp.logical_and(z + d < n, z > 0))
            def _(d=d, i=i):
                down(d, i).start()

    out_ref[z] = x_ref[...]
    for i in range(k):
        arrived(n - 1, i)
    for d in range(n - 1):
        for i in range(k):

            @pl.when(jnp.logical_and(z >= d, z < n - 1))
            def _(d=d, i=i):
                up(d, i).wait_send()

            @pl.when(jnp.logical_and(z + d < n, z > 0))
            def _(d=d, i=i):
                down(d, i).wait_send()


def call(kernel, outs, scratch, name, *args):
    return pl.pallas_call(
        kernel,
        out_shape=outs,
        in_specs=[pl.BlockSpec(memory_space=pltpu.VMEM)] * len(args),
        out_specs=jax.tree.map(lambda _: pl.BlockSpec(memory_space=pltpu.VMEM), outs),
        scratch_shapes=scratch,
        compiler_params=pltpu.CompilerParams(has_side_effects=True, vmem_limit_bytes=32 * 2**20),
        name=name,
    )(*args)


def by_kernels(clip_feats, proj_weight):
    pairs = clip_feats.shape[1]
    width = clip_feats.shape[2]
    depth = proj_weight.shape[0]
    n, m = lax.axis_size("dp"), lax.axis_size("feat")
    parts = m // n
    total = pairs * n
    pair_count = float(total)
    columns = width // n
    piece = 2 * pairs // n
    f32, bf16 = jnp.float32, jnp.bfloat16
    rows = call(
        functools.partial(rows_kernel, n, parts),
        jax.ShapeDtypeStruct((parts, n, n, piece, width), bf16),
        [pltpu.VMEM((n, piece, width), bf16), DMA((2,))]
        + [DMA((n,))] * 4
        + [DMA((n, n))] * 2
        + [DMA((parts, n, n))] * 2,
        "rows",
        clip_feats.reshape(n, piece, width),
    ).reshape(parts, 2 * total, width)
    partial = sum(
        jnp.dot(rows[i], proj_weight[i * width : (i + 1) * width], preferred_element_type=f32)
        for i in range(parts)
    ).reshape(2, total, width)
    partial = (partial - jnp.mean(partial, axis=1, keepdims=True)).astype(bf16)
    pieces = jnp.stack([partial[:, :, i * columns : (i + 1) * columns] for i in range(n)])
    k = cuts
    centered = call(
        functools.partial(sums_kernel, n, k),
        jax.ShapeDtypeStruct((k, 2 * total // k, columns), f32),
        [pltpu.VMEM((n, k, 2 * total // k, columns), bf16)] * 3 + [DMA((n, k))] * 4,
        "sums",
        pieces.reshape(n, k, 2 * total // k, columns),
    ).reshape(2, total, columns)
    col_var = jnp.mean(centered * centered, axis=1, keepdims=True)
    col_scale = lax.rsqrt(col_var + epsilon)
    normed = centered * col_scale
    quantized = normed.astype(bf16)
    widened = quantized.astype(f32)
    gram_part = jnp.einsum("vpc,vnc->vpn", quantized, quantized, preferred_element_type=f32)
    diag_corr = jnp.sum(widened[0] * widened[1], axis=0) / pair_count
    diag_part = jnp.sum((1.0 - diag_corr) ** 2 - off_weight * diag_corr * diag_corr)
    square_part = jnp.sum(diag_corr * diag_corr)
    lane = lax.broadcasted_iota(jnp.int32, (8, 128), 1)
    small = jnp.where(lane == 0, diag_part, jnp.where(lane == 1, square_part, 0.0))
    block = 2 * total // m
    gram_q, small = call(
        functools.partial(gram_kernel, n, m),
        (jax.ShapeDtypeStruct((m, block, total), bf16), jax.ShapeDtypeStruct((8, 128), f32)),
        [
            pltpu.VMEM((m, block, total), bf16),
            pltpu.VMEM((m, 8, 128), f32),
            pltpu.VMEM((block, total), bf16),
            pltpu.VMEM((8, 128), f32),
            pltpu.VMEM((n, block, total), bf16),
            pltpu.VMEM((n, 8, 128), f32),
        ]
        + [DMA((m,))] * 4
        + [DMA((n,))] * 4
        + [DMA((m,))] * 2,
        "grams",
        gram_part.astype(bf16).reshape(m, block, total),
        small,
    )
    gram_q = gram_q.reshape(2, total, total)
    slope = -2.0 * (1.0 - diag_corr) - 2.0 * off_weight * diag_corr
    coefficient = 2.0 * off_weight / (pair_count * pair_count)
    cross_first = jnp.dot(gram_q[1], quantized[0], preferred_element_type=f32)
    cross_second = jnp.dot(gram_q[0], quantized[1], preferred_element_type=f32)
    grad_norm = jnp.stack(
        [
            slope * widened[1] / pair_count + coefficient * cross_first,
            slope * widened[0] / pair_count + coefficient * cross_second,
        ]
    )
    mean_one = jnp.mean(grad_norm, axis=1, keepdims=True)
    mean_two = jnp.mean(grad_norm * normed, axis=1, keepdims=True)
    pre_q = (col_scale * (grad_norm - mean_one - normed * mean_two)).astype(bf16)
    flat_grad = call(
        functools.partial(column_kernel, n, k),
        jax.ShapeDtypeStruct((n, k, 2 * total // k, columns), bf16),
        [DMA((n, k))] * 4,
        "columns",
        pre_q.reshape(k, 2 * total // k, columns),
    ).reshape(n, 2 * total, columns)
    flat_grad = jnp.concatenate([flat_grad[i] for i in range(n)], axis=1)
    summed = jnp.einsum("crk,rw->ckw", rows, flat_grad, preferred_element_type=f32)
    weight_grad = grad_scale * summed.reshape(depth, width)
    grams = gram_q.astype(f32)
    frob_scaled = jnp.sum(grams[0] * grams[1]) / (pair_count * pair_count)
    loss_value = 16.0 * (small[0, 0] + off_weight * frob_scaled) / float(D)
    redundancy = 8.0 * pair_count * (frob_scaled - small[0, 1]) / (float(D) * float(D))
    half = n // 2
    z = lax.axis_index("dp")
    own = grams.reshape(2, half, n, piece, total)
    own = lax.dynamic_slice_in_dim(own, z, 1, axis=2)
    own = (own[0] + own[1]).reshape(pairs, half, n, piece).transpose(0, 2, 1, 3).reshape(pairs, total)
    row_ids = lax.broadcasted_iota(jnp.int32, (pairs, total), 0) + z * pairs
    col_ids = lax.broadcasted_iota(jnp.int32, (pairs, total), 1)
    pair_similarity = jnp.where(row_ids == col_ids, 0.0, own / (2.0 * math.sqrt(float(D))))
    return (loss_value, weight_grad, redundancy, pair_similarity)


def by_collectives(clip_feats, proj_weight):
    pairs = clip_feats.shape[1]
    width = clip_feats.shape[2]
    depth = proj_weight.shape[0]
    dp_count = lax.axis_size("dp")
    total = pairs * dp_count
    pair_count = float(total)
    gathered = lax.all_gather(clip_feats, "feat", axis=0, tiled=False)
    rows = lax.all_to_all(gathered, "dp", split_axis=0, concat_axis=0, tiled=True)
    parts = depth // width
    rows = rows.reshape(dp_count, parts, 2 * pairs, width).transpose(1, 0, 2, 3)
    rows = rows.reshape(parts, 2 * total, width)
    partial = sum(
        jnp.dot(rows[i], proj_weight[i * width : (i + 1) * width], preferred_element_type=jnp.float32)
        for i in range(parts)
    ).reshape(dp_count, 2, pairs, width)
    partial = partial - jnp.mean(partial, axis=(0, 2), keepdims=True)
    columns = width // dp_count
    pieces = partial.astype(jnp.bfloat16).reshape(2 * total, width)
    pieces = jnp.stack([pieces[:, i * columns : (i + 1) * columns] for i in range(dp_count)])
    pieces = lax.all_to_all(pieces, "dp", split_axis=0, concat_axis=0, tiled=True)
    centered = jnp.sum(pieces.astype(jnp.float32), axis=0)
    centered = centered.reshape(dp_count, 2, pairs, columns).transpose(1, 0, 2, 3).reshape(2, total, columns)
    col_var = jnp.mean(centered * centered, axis=1, keepdims=True)
    col_scale = lax.rsqrt(col_var + epsilon)
    normed = centered * col_scale
    quantized = normed.astype(jnp.bfloat16)
    widened = quantized.astype(jnp.float32)
    gram_part = jnp.einsum("vpc,vnc->vpn", quantized, quantized, preferred_element_type=jnp.float32)
    diag_corr = jnp.sum(widened[0] * widened[1], axis=0) / pair_count
    diag_part = jnp.sum((1.0 - diag_corr) ** 2 - off_weight * diag_corr * diag_corr)
    square_part = jnp.sum(diag_corr * diag_corr)
    grams, diag_term, squares = lax.psum((gram_part, diag_part, square_part), ("dp", "feat"))
    frob_scaled = jnp.sum(grams[0] * grams[1]) / (pair_count * pair_count)
    loss_value = 16.0 * (diag_term + off_weight * frob_scaled) / float(D)
    redundancy = 8.0 * pair_count * (frob_scaled - squares) / (float(D) * float(D))
    first_row = lax.axis_index("dp") * pairs
    own = lax.dynamic_slice_in_dim(grams, first_row, pairs, axis=1)
    row_ids = lax.broadcasted_iota(jnp.int32, (pairs, total), 0) + first_row
    col_ids = lax.broadcasted_iota(jnp.int32, (pairs, total), 1)
    pair_similarity = jnp.where(
        row_ids == col_ids, 0.0, (own[0] + own[1]) / (2.0 * math.sqrt(float(D)))
    )
    slope = -2.0 * (1.0 - diag_corr) - 2.0 * off_weight * diag_corr
    coefficient = 2.0 * off_weight / (pair_count * pair_count)
    gram_q = grams.astype(jnp.bfloat16)
    cross_first = jnp.dot(gram_q[1], quantized[0], preferred_element_type=jnp.float32)
    cross_second = jnp.dot(gram_q[0], quantized[1], preferred_element_type=jnp.float32)
    grad_norm = jnp.stack(
        [
            slope * widened[1] / pair_count + coefficient * cross_first,
            slope * widened[0] / pair_count + coefficient * cross_second,
        ]
    )
    mean_one = jnp.mean(grad_norm, axis=1, keepdims=True)
    mean_two = jnp.mean(grad_norm * normed, axis=1, keepdims=True)
    pre_q = (col_scale * (grad_norm - mean_one - normed * mean_two)).astype(jnp.bfloat16)
    pre_q = pre_q.reshape(2, dp_count, pairs, columns).transpose(1, 0, 2, 3).reshape(2 * total, columns)
    flat_grad = lax.all_gather(pre_q, "dp", axis=1, tiled=True)
    summed = jnp.concatenate(
        [jnp.dot(rows[i].T, flat_grad, preferred_element_type=jnp.float32) for i in range(parts)]
    )
    return (loss_value, grad_scale * summed, redundancy, pair_similarity)


def per_device(clip_feats, proj_weight):
    pairs, width = clip_feats.shape[1:]
    n, m = lax.axis_size("dp"), lax.axis_size("feat")
    aligned = n % 2 == 0 and m % n == 0 and m > n and proj_weight.shape[0] == width * (m // n)
    aligned = aligned and width % (128 * n) == 0 and (2 * pairs) % (16 * n) == 0
    aligned = aligned and (2 * pairs * n) % (16 * m) == 0
    aligned = aligned and (2 * pairs * n) % (16 * cuts) == 0
    return (by_kernels if aligned else by_collectives)(clip_feats, proj_weight)


def solution(mesh):
    placed = (P(None, "dp", "feat"), P("dp", "feat"))
    return jax.shard_map(
        per_device,
        mesh=mesh,
        in_specs=placed,
        out_specs=(P(), P("dp", "feat"), P(), P("dp", None)),
        check_vma=False,
    )
```

```python
import functools
import math

import jax
import jax.numpy as jnp
from jax import lax
from jax.experimental import pallas as pl
from jax.experimental.pallas import tpu as pltpu
from jax.sharding import PartitionSpec as P

D = 8192


off_weight = 0.0051
epsilon = 1e-05
grad_scale = 32.0
cuts = 8

MESH = pl.DeviceIdType.MESH
DMA = pltpu.SemaphoreType.DMA


def remote(src, dst, send_sem, recv_sem, dp, feat):
    return pltpu.make_async_remote_copy(
        src_ref=src,
        dst_ref=dst,
        send_sem=send_sem,
        recv_sem=recv_sem,
        device_id=(dp, feat),
        device_id_type=MESH,
    )


def rows_kernel(
    n, parts, x_ref, out_ref, mid, local, send_a, recv_a, send_b, recv_b, send_c, recv_c, send_d, recv_d
):
    z, f = lax.axis_index("dp"), lax.axis_index("feat")
    q, c = lax.div(f, parts), lax.rem(f, parts)
    spread = []
    for d in range(1, n):
        to = lax.rem(q + d, n)
        spread.append(remote(x_ref.at[to], mid.at[q], send_a.at[d], recv_a.at[d], z, to * parts + c))
    for copy in spread:
        copy.start()
    kept = pltpu.make_async_copy(x_ref.at[q], mid.at[q], local.at[0])
    kept.start()
    kept.wait()
    for d in range(n):
        s = lax.rem(q + n - d, n)
        if d > 0:
            spread[d - 1].wait_recv()

        @pl.when(z != s)
        def _(d=d, s=s):
            remote(mid.at[s], out_ref.at[c, q, z], send_b.at[d], recv_b.at[z], s, f).start()

        @pl.when(z == s)
        def _(s=s):
            own = pltpu.make_async_copy(mid.at[s], out_ref.at[c, q, z], local.at[1])
            own.start()
            own.wait()

    def across(d, e):
        block = out_ref.at[c, lax.rem(q + n - d, n), lax.rem(z + e, n)]
        return [
            remote(block, block, send_d.at[i, d, e], recv_d.at[i, d, e], z, q * parts + lax.rem(c + i, parts))
            for i in range(1, parts)
        ]

    ring, pairs = {}, []
    for e in range(n):
        s = lax.rem(z + e, n)
        mine = out_ref.at[c, q, s]
        if e > 0:
            remote(x_ref.at[0], mine, send_b.at[0], recv_b.at[s], z, f).wait_recv()
        for d in range(1, n):
            to = lax.rem(q + d, n) * parts + c
            ring[d, e] = remote(mine, mine, send_c.at[d, e], recv_c.at[d, e], z, to)
            ring[d, e].start()
        passed = across(0, e)
        for copy in passed:
            copy.start()
        pairs += passed
    for e in range(n):
        for d in range(1, n):
            ring[d, e].wait_recv()
            passed = across(d, e)
            for copy in passed:
                copy.start()
            pairs += passed
    for copy in pairs:
        copy.wait()
    for copy in list(ring.values()) + spread:
        copy.wait_send()
    for d in range(n):
        s = lax.rem(q + n - d, n)

        @pl.when(z != s)
        def _(d=d, s=s):
            remote(mid.at[s], out_ref.at[c, q, z], send_b.at[d], recv_b.at[z], s, f).wait_send()


def sums_kernel(n, k, x_ref, out_ref, sums, above, below, send_up, recv_up, send_down, recv_down):
    z, f = lax.axis_index("dp"), lax.axis_index("feat")

    def step(t, i, start, rising):
        first = z == (0 if rising else n - 1)
        active = z < t if rising else z > t
        got = below if rising else above
        send, recv = (send_up, recv_up) if rising else (send_down, recv_down)
        to = z + 1 if rising else z - 1

        @pl.when(jnp.logical_and(active, first))
        def _():
            copy = remote(x_ref.at[t, i], got.at[t, i], send.at[t, i], recv.at[t, i], to, f)
            order = (n - 1 - t if rising else t) * k + i
            if start:
                copy.start()
                if order >= 2:
                    j, b = divmod(order - 2, k)
                    a = n - 1 - j if rising else j
                    remote(x_ref.at[a, b], got.at[a, b], send.at[a, b], recv.at[a, b], to, f).wait_send()
            elif order >= (n - 1) * k - 2:
                copy.wait_send()

        @pl.when(jnp.logical_and(active, jnp.logical_not(first)))
        def _():
            copy = remote(sums.at[t, i], got.at[t, i], send.at[t, i], recv.at[t, i], to, f)
            if start:
                copy.wait_recv()
                total = x_ref[t, i].astype(jnp.float32) + got[t, i].astype(jnp.float32)
                sums[t, i] = total.astype(sums.dtype)
                copy.start()
            else:
                copy.wait_send()

    for j in range(n - 1):
        for i in range(k):
            step(n - 1 - j, i, True, True)
            step(j, i, True, False)
    out_ref[...] = x_ref[z].astype(jnp.float32)
    for i in range(k):

        @pl.when(z > 0)
        def _(i=i):
            remote(x_ref.at[0, i], below.at[z, i], send_up.at[0, i], recv_up.at[z, i], z, f).wait_recv()
            out_ref[i] += below[z, i].astype(jnp.float32)

        @pl.when(z < n - 1)
        def _(i=i):
            remote(x_ref.at[0, i], above.at[z, i], send_down.at[0, i], recv_down.at[z, i], z, f).wait_recv()
            out_ref[i] += above[z, i].astype(jnp.float32)

    for j in range(n - 1):
        for i in range(k):
            step(n - 1 - j, i, False, True)
            step(j, i, False, False)


def gram_kernel(
    n, m, g_ref, s_ref, out_ref, total_ref, plane, scalars, mid, scalar_mid, column, scalar_column,
    send_a, recv_a, send_b, recv_b, send_c, recv_c, send_d, recv_d, send_e, recv_e,
):
    z, f = lax.axis_index("dp"), lax.axis_index("feat")
    started = []
    for d in range(1, m):
        to = lax.rem(f + d, m)
        started.append(remote(g_ref.at[to], plane.at[f], send_a.at[d], recv_a.at[d], z, to))
        started.append(remote(s_ref, scalars.at[f], send_b.at[d], recv_b.at[d], z, to))
    for copy in started:
        copy.start()
    plane[f] = g_ref[f]
    scalars[f] = s_ref[...]
    for copy in started:
        copy.wait()
    total = plane[0].astype(jnp.float32)
    for i in range(1, m):
        total += plane[i].astype(jnp.float32)
    mid[...] = total.astype(mid.dtype)
    small = scalars[0]
    for i in range(1, m):
        small += scalars[i]
    scalar_mid[...] = small
    started = []
    for d in range(1, n):
        to = lax.rem(z + d, n)
        started.append(remote(mid, column.at[z], send_c.at[d], recv_c.at[d], to, f))
        started.append(remote(scalar_mid, scalar_column.at[z], send_d.at[d], recv_d.at[d], to, f))
    for copy in started:
        copy.start()
    column[z] = mid[...]
    scalar_column[z] = scalar_mid[...]
    for copy in started:
        copy.wait()
    total = column[0].astype(jnp.float32)
    for i in range(1, n):
        total += column[i].astype(jnp.float32)
    out_ref[f] = total.astype(out_ref.dtype)
    small = scalar_column[0]
    for i in range(1, n):
        small += scalar_column[i]
    total_ref[...] = small
    started = [
        remote(out_ref.at[f], out_ref.at[f], send_e.at[d], recv_e.at[d], z, lax.rem(f + d, m))
        for d in range(1, m)
    ]
    for copy in started:
        copy.start()
    for copy in started:
        copy.wait()


def column_kernel(n, k, x_ref, out_ref, send_up, recv_up, send_down, recv_down):
    z, f = lax.axis_index("dp"), lax.axis_index("feat")

    def up(d, i):
        where = out_ref.at[z - d, i]
        src = x_ref.at[i] if d == 0 else where
        return remote(src, where, send_up.at[d, i], recv_up.at[d, i], z + 1, f)

    def down(d, i):
        where = out_ref.at[z + d, i]
        src = x_ref.at[i] if d == 0 else where
        return remote(src, where, send_down.at[d, i], recv_down.at[d, i], z - 1, f)

    def arrived(d, i):
        @pl.when(z >= d)
        def _():
            remote(x_ref.at[i], out_ref.at[z - d, i], send_up.at[0, i], recv_up.at[d - 1, i], z, f).wait_recv()

        @pl.when(z + d < n)
        def _():
            remote(x_ref.at[i], out_ref.at[z + d, i], send_down.at[0, i], recv_down.at[d - 1, i], z, f).wait_recv()

    for d in range(n - 1):
        for i in range(k):
            if d > 0:
                arrived(d, i)

            @pl.when(jnp.logical_and(z >= d, z < n - 1))
            def _(d=d, i=i):
                up(d, i).start()

            @pl.when(jnp.logical_and(z + d < n, z > 0))
            def _(d=d, i=i):
                down(d, i).start()

    out_ref[z] = x_ref[...]
    for i in range(k):
        arrived(n - 1, i)
    for d in range(n - 1):
        for i in range(k):

            @pl.when(jnp.logical_and(z >= d, z < n - 1))
            def _(d=d, i=i):
                up(d, i).wait_send()

            @pl.when(jnp.logical_and(z + d < n, z > 0))
            def _(d=d, i=i):
                down(d, i).wait_send()


def call(kernel, outs, scratch, name, *args):
    return pl.pallas_call(
        kernel,
        out_shape=outs,
        in_specs=[pl.BlockSpec(memory_space=pltpu.VMEM)] * len(args),
        out_specs=jax.tree.map(lambda _: pl.BlockSpec(memory_space=pltpu.VMEM), outs),
        scratch_shapes=scratch,
        compiler_params=pltpu.CompilerParams(has_side_effects=True, vmem_limit_bytes=32 * 2**20),
        name=name,
    )(*args)


def by_kernels(clip_feats, proj_weight):
    pairs = clip_feats.shape[1]
    width = clip_feats.shape[2]
    depth = proj_weight.shape[0]
    n, m = lax.axis_size("dp"), lax.axis_size("feat")
    parts = m // n
    total = pairs * n
    pair_count = float(total)
    columns = width // n
    piece = 2 * pairs // n
    f32, bf16 = jnp.float32, jnp.bfloat16
    rows = call(
        functools.partial(rows_kernel, n, parts),
        jax.ShapeDtypeStruct((parts, n, n, piece, width), bf16),
        [pltpu.VMEM((n, piece, width), bf16), DMA((2,))]
        + [DMA((n,))] * 4
        + [DMA((n, n))] * 2
        + [DMA((parts, n, n))] * 2,
        "rows",
        clip_feats.reshape(n, piece, width),
    ).reshape(parts, 2 * total, width)
    partial = sum(
        jnp.dot(rows[i], proj_weight[i * width : (i + 1) * width], preferred_element_type=f32)
        for i in range(parts)
    ).reshape(2, total, width)
    partial = (partial - jnp.mean(partial, axis=1, keepdims=True)).astype(bf16)
    pieces = jnp.stack([partial[:, :, i * columns : (i + 1) * columns] for i in range(n)])
    k = cuts
    centered = call(
        functools.partial(sums_kernel, n, k),
        jax.ShapeDtypeStruct((k, 2 * total // k, columns), f32),
        [pltpu.VMEM((n, k, 2 * total // k, columns), bf16)] * 3 + [DMA((n, k))] * 4,
        "sums",
        pieces.reshape(n, k, 2 * total // k, columns),
    ).reshape(2, total, columns)
    col_var = jnp.mean(centered * centered, axis=1, keepdims=True)
    col_scale = lax.rsqrt(col_var + epsilon)
    normed = centered * col_scale
    quantized = normed.astype(bf16)
    widened = quantized.astype(f32)
    gram_part = jnp.einsum("vpc,vnc->vpn", quantized, quantized, preferred_element_type=f32)
    diag_corr = jnp.sum(widened[0] * widened[1], axis=0) / pair_count
    diag_part = jnp.sum((1.0 - diag_corr) ** 2 - off_weight * diag_corr * diag_corr)
    square_part = jnp.sum(diag_corr * diag_corr)
    lane = lax.broadcasted_iota(jnp.int32, (8, 128), 1)
    small = jnp.where(lane == 0, diag_part, jnp.where(lane == 1, square_part, 0.0))
    block = 2 * total // m
    gram_q, small = call(
        functools.partial(gram_kernel, n, m),
        (jax.ShapeDtypeStruct((m, block, total), bf16), jax.ShapeDtypeStruct((8, 128), f32)),
        [
            pltpu.VMEM((m, block, total), bf16),
            pltpu.VMEM((m, 8, 128), f32),
            pltpu.VMEM((block, total), bf16),
            pltpu.VMEM((8, 128), f32),
            pltpu.VMEM((n, block, total), bf16),
            pltpu.VMEM((n, 8, 128), f32),
        ]
        + [DMA((m,))] * 4
        + [DMA((n,))] * 4
        + [DMA((m,))] * 2,
        "grams",
        gram_part.astype(bf16).reshape(m, block, total),
        small,
    )
    gram_q = gram_q.reshape(2, total, total)
    slope = -2.0 * (1.0 - diag_corr) - 2.0 * off_weight * diag_corr
    coefficient = 2.0 * off_weight / (pair_count * pair_count)
    cross_first = jnp.dot(gram_q[1], quantized[0], preferred_element_type=f32)
    cross_second = jnp.dot(gram_q[0], quantized[1], preferred_element_type=f32)
    grad_norm = jnp.stack(
        [
            slope * widened[1] / pair_count + coefficient * cross_first,
            slope * widened[0] / pair_count + coefficient * cross_second,
        ]
    )
    mean_one = jnp.mean(grad_norm, axis=1, keepdims=True)
    mean_two = jnp.mean(grad_norm * normed, axis=1, keepdims=True)
    pre_q = (col_scale * (grad_norm - mean_one - normed * mean_two)).astype(bf16)
    flat_grad = call(
        functools.partial(column_kernel, n, k),
        jax.ShapeDtypeStruct((n, k, 2 * total // k, columns), bf16),
        [DMA((n, k))] * 4,
        "columns",
        pre_q.reshape(k, 2 * total // k, columns),
    ).reshape(n, 2 * total, columns)
    flat_grad = jnp.concatenate([flat_grad[i] for i in range(n)], axis=1)
    summed = jnp.einsum("crk,rw->ckw", rows, flat_grad, preferred_element_type=f32)
    weight_grad = grad_scale * summed.reshape(depth, width)
    grams = gram_q.astype(f32)
    frob_scaled = jnp.sum(grams[0] * grams[1]) / (pair_count * pair_count)
    loss_value = 16.0 * (small[0, 0] + off_weight * frob_scaled) / float(D)
    redundancy = 8.0 * pair_count * (frob_scaled - small[0, 1]) / (float(D) * float(D))
    half = n // 2
    z = lax.axis_index("dp")
    own = grams.reshape(2, half, n, piece, total)
    own = lax.dynamic_slice_in_dim(own, z, 1, axis=2)
    own = (own[0] + own[1]).reshape(pairs, half, n, piece).transpose(0, 2, 1, 3).reshape(pairs, total)
    row_ids = lax.broadcasted_iota(jnp.int32, (pairs, total), 0) + z * pairs
    col_ids = lax.broadcasted_iota(jnp.int32, (pairs, total), 1)
    pair_similarity = jnp.where(row_ids == col_ids, 0.0, own / (2.0 * math.sqrt(float(D))))
    return (loss_value, weight_grad, redundancy, pair_similarity)


def by_collectives(clip_feats, proj_weight):
    pairs = clip_feats.shape[1]
    width = clip_feats.shape[2]
    depth = proj_weight.shape[0]
    dp_count = lax.axis_size("dp")
    total = pairs * dp_count
    pair_count = float(total)
    gathered = lax.all_gather(clip_feats, "feat", axis=0, tiled=False)
    rows = lax.all_to_all(gathered, "dp", split_axis=0, concat_axis=0, tiled=True)
    parts = depth // width
    rows = rows.reshape(dp_count, parts, 2 * pairs, width).transpose(1, 0, 2, 3)
    rows = rows.reshape(parts, 2 * total, width)
    partial = sum(
        jnp.dot(rows[i], proj_weight[i * width : (i + 1) * width], preferred_element_type=jnp.float32)
        for i in range(parts)
    ).reshape(dp_count, 2, pairs, width)
    partial = partial - jnp.mean(partial, axis=(0, 2), keepdims=True)
    columns = width // dp_count
    pieces = partial.astype(jnp.bfloat16).reshape(2 * total, width)
    pieces = jnp.stack([pieces[:, i * columns : (i + 1) * columns] for i in range(dp_count)])
    pieces = lax.all_to_all(pieces, "dp", split_axis=0, concat_axis=0, tiled=True)
    centered = jnp.sum(pieces.astype(jnp.float32), axis=0)
    centered = centered.reshape(dp_count, 2, pairs, columns).transpose(1, 0, 2, 3).reshape(2, total, columns)
    col_var = jnp.mean(centered * centered, axis=1, keepdims=True)
    col_scale = lax.rsqrt(col_var + epsilon)
    normed = centered * col_scale
    quantized = normed.astype(jnp.bfloat16)
    widened = quantized.astype(jnp.float32)
    gram_part = jnp.einsum("vpc,vnc->vpn", quantized, quantized, preferred_element_type=jnp.float32)
    diag_corr = jnp.sum(widened[0] * widened[1], axis=0) / pair_count
    diag_part = jnp.sum((1.0 - diag_corr) ** 2 - off_weight * diag_corr * diag_corr)
    square_part = jnp.sum(diag_corr * diag_corr)
    grams, diag_term, squares = lax.psum((gram_part, diag_part, square_part), ("dp", "feat"))
    frob_scaled = jnp.sum(grams[0] * grams[1]) / (pair_count * pair_count)
    loss_value = 16.0 * (diag_term + off_weight * frob_scaled) / float(D)
    redundancy = 8.0 * pair_count * (frob_scaled - squares) / (float(D) * float(D))
    first_row = lax.axis_index("dp") * pairs
    own = lax.dynamic_slice_in_dim(grams, first_row, pairs, axis=1)
    row_ids = lax.broadcasted_iota(jnp.int32, (pairs, total), 0) + first_row
    col_ids = lax.broadcasted_iota(jnp.int32, (pairs, total), 1)
    pair_similarity = jnp.where(
        row_ids == col_ids, 0.0, (own[0] + own[1]) / (2.0 * math.sqrt(float(D)))
    )
    slope = -2.0 * (1.0 - diag_corr) - 2.0 * off_weight * diag_corr
    coefficient = 2.0 * off_weight / (pair_count * pair_count)
    gram_q = grams.astype(jnp.bfloat16)
    cross_first = jnp.dot(gram_q[1], quantized[0], preferred_element_type=jnp.float32)
    cross_second = jnp.dot(gram_q[0], quantized[1], preferred_element_type=jnp.float32)
    grad_norm = jnp.stack(
        [
            slope * widened[1] / pair_count + coefficient * cross_first,
            slope * widened[0] / pair_count + coefficient * cross_second,
        ]
    )
    mean_one = jnp.mean(grad_norm, axis=1, keepdims=True)
    mean_two = jnp.mean(grad_norm * normed, axis=1, keepdims=True)
    pre_q = (col_scale * (grad_norm - mean_one - normed * mean_two)).astype(jnp.bfloat16)
    pre_q = pre_q.reshape(2, dp_count, pairs, columns).transpose(1, 0, 2, 3).reshape(2 * total, columns)
    flat_grad = lax.all_gather(pre_q, "dp", axis=1, tiled=True)
    summed = jnp.concatenate(
        [jnp.dot(rows[i].T, flat_grad, preferred_element_type=jnp.float32) for i in range(parts)]
    )
    return (loss_value, grad_scale * summed, redundancy, pair_similarity)


def per_device(clip_feats, proj_weight):
    pairs, width = clip_feats.shape[1:]
    n, m = lax.axis_size("dp"), lax.axis_size("feat")
    aligned = n % 2 == 0 and m % n == 0 and m > n and proj_weight.shape[0] == width * (m // n)
    aligned = aligned and width % (128 * n) == 0 and (2 * pairs) % (16 * n) == 0
    aligned = aligned and (2 * pairs * n) % (16 * m) == 0
    aligned = aligned and (2 * pairs * n) % (16 * cuts) == 0
    return (by_kernels if aligned else by_collectives)(clip_feats, proj_weight)


def solution(mesh):
    placed = (P(None, "dp", "feat"), P("dp", "feat"))
    return jax.shard_map(
        per_device,
        mesh=mesh,
        in_specs=placed,
        out_specs=(P(), P("dp", "feat"), P(), P("dp", None)),
        check_vma=False,
    )
```
